32 devices in a mesh: wrap: 8 (over z, y), samp: 4 (over x, core).
Axes of the slice: x: 2, y: 2, z: 4, core: 2. Of those that a mesh axis runs over, the one named last changes fastest.
Arguments:
- inputs: bfloat16 [4, 64, 64, 256], P('samp', None, 'wrap'), may hold values from -6 to 6
- cotangent: bfloat16 [4, 64, 64, 256], P('samp', None, 'wrap'), may hold values from -6 to 6
- weight_one: bfloat16 [64, 1728], replicated, may hold values from -0.15625 to 0.15625
- bias_one: float32 [64], replicated, may hold values from -3 to 3
- weight_two: bfloat16 [64, 1728], replicated, may hold values from -0.15625 to 0.15625
- bias_two: float32 [64], replicated, may hold values from -3 to 3
- dilation: int32 [2], replicated, may hold values from 1 to 4, as said below
Outputs:
- prediction: bfloat16 [4, 64, 64, 256], P('samp', None, 'wrap')
- grad_weight_one: float32 [64, 1728], replicated
- grad_bias_one: float32 [64], replicated
- grad_weight_two: float32 [64, 1728], replicated
- grad_bias_two: float32 [64], replicated
The draws below stay inside these ranges and needn't reach their ends.
Inputs may be any that keep to these rules, and one draw needn't show every extreme that they name: `dilation`: in every draw one of the two rates equals 4.
All inputs are finite; a program needn't handle non-finite values.
Results may differ from the reference program's by a relative error of at most 0.006.
Values may be sent and summed in bfloat16 or wider, within the bound.
No kernel may reach another device: no remote copies, remote signals or barrier semaphores. Data moves between devices by JAX's collectives and lax.ppermute only.
A program may use at most 128 MiB of HBM per device.

```python
import math
import jax
import jax.numpy as jnp
from jax import lax

C = 64
DMAX = 4
NR = 16
S = 16
WRAP = 64
NS = 256
SAMPLES = 4


def draw_dilation(key, part):
    keys = jax.random.split(key, 2)
    other = jax.random.randint(keys[0], (), 1, DMAX + 1).astype(jnp.int32)
    which = jax.random.randint(keys[1], (), 0, 2)
    top = jnp.full((), DMAX, jnp.int32)
    return jnp.where(which == 0, jnp.stack([top, other]), jnp.stack([other, top])).astype(jnp.int32)


def level_of(rng, extent, shards, least, high):
    def one(position, parts):
        steps = jax.random.uniform(jax.random.fold_in(jax.random.fold_in(rng, 6), position), (parts,), jnp.float32, least / len(shards), high / len(shards))
        return jnp.repeat(jnp.exp(steps), extent[position] // parts).reshape((-1,) + (1,) * (len(extent) - position - 1))

    level = one(*shards[0])
    for cut in shards[1:]:
        level = level * one(*cut)
    return level


def scatter_about(stream_key, shape, spread, limit, pieces=(), kind=jnp.bfloat16):
    result = jax.random.normal(stream_key, shape, jnp.float32) * spread
    if len(pieces) > 0:
        result = level_of(stream_key, shape, pieces, -0.22, 0.18) * result
    return jnp.clip(result, min=-limit, max=limit).astype(kind)


def setup_inputs(seed: int = 0) -> dict:
    splits = jax.random.split(jax.random.key(seed), 8)
    inputs = scatter_about(splits[0], (SAMPLES, C, WRAP, NS), 1.0, 6.0, ((0, 4), (2, 8)))
    cotangent = scatter_about(splits[1], (SAMPLES, C, WRAP, NS), 1.0, 6.0, ((0, 4), (2, 8)))
    weight_one = scatter_about(splits[2], (C, 27 * C), (27 * C) ** -0.5, 0.15625)
    bias_one = scatter_about(splits[3], (C,), 0.5, 3.0, (), jnp.float32)
    weight_two = scatter_about(splits[4], (C, 27 * C), (27 * C) ** -0.5, 0.15625)
    bias_two = scatter_about(splits[5], (C,), 0.5, 3.0, (), jnp.float32)
    dilation = draw_dilation(jax.random.fold_in(splits[7], 71), 0)
    return dict(inputs=inputs, cotangent=cotangent, weight_one=weight_one, bias_one=bias_one, weight_two=weight_two, bias_two=bias_two, dilation=dilation)


def grid_of(field, margin):
    chans = field.shape[0]
    shaped = field.reshape(chans, field.shape[1], NR, S)
    return jnp.pad(shaped, ((0, 0), (0, 0), (DMAX, DMAX), (DMAX, DMAX)))

def tap_stack(padded, rate, first_row, out_rows, tap_w):
    in_chan = padded.shape[0]
    anchor = jnp.zeros((), jnp.int32)
    windows = []
    for tap_n in range(3):
        for tap_s in range(3):
            offsets = (anchor, (first_row + (tap_w - 1) * rate).astype(jnp.int32), (DMAX + (tap_n - 1) * rate).astype(jnp.int32), (DMAX + (tap_s - 1) * rate).astype(jnp.int32))
            window = lax.dynamic_slice(padded, offsets, (in_chan, out_rows, NR, S))
            windows.append(window.reshape(in_chan, -1))
    return jnp.concatenate(windows, 0)

def convolve(padded, weight, rate, first_row, out_rows):
    in_chan = padded.shape[0]
    summed = None
    for tap_w in range(3):
        stacked = tap_stack(padded, rate, first_row, out_rows, tap_w)
        term = jnp.dot(weight[:, tap_w * 9 * in_chan:(tap_w + 1) * 9 * in_chan], stacked, preferred_element_type=jnp.float32)
        summed = term if summed is None else summed + term
    return summed

def weight_grad(cot, padded, rate, first_row, out_rows):
    columns = []
    for tap_w in range(3):
        stacked = tap_stack(padded, rate, first_row, out_rows, tap_w)
        columns.append(lax.dot_general(cot, stacked, (((1,), (1,)), ((), ())), preferred_element_type=jnp.float32))
    return jnp.concatenate(columns, 1)

def flip_kernel(weight):
    chans = weight.shape[0]
    shaped = weight.reshape(chans, 27, chans)[:, ::-1, :]
    return jnp.transpose(shaped, (2, 1, 0)).reshape(chans, 27 * chans)

def cycle_pad(field):
    return jnp.concatenate([field[:, -DMAX:], field, field[:, :DMAX]], 1)

def reference(inputs, cotangent, weight_one, bias_one, weight_two, bias_two, dilation):
    first_rate = dilation[0]
    second_rate = dilation[1]
    flipped = flip_kernel(weight_two)
    chans = inputs.shape[1]
    rows = inputs.shape[2]

    def one_sample(pair):
        sample, cot = pair
        grid_in = grid_of(cycle_pad(sample), DMAX)
        pre_one = convolve(grid_in, weight_one, first_rate, DMAX, rows) + bias_one[:, None]
        hidden = jax.nn.silu(pre_one).astype(jnp.bfloat16).reshape(chans, rows, -1)
        grid_hidden = grid_of(cycle_pad(hidden), DMAX)
        output = (convolve(grid_hidden, weight_two, second_rate, DMAX, rows) + bias_two[:, None]).astype(jnp.bfloat16)
        cot_flat = cot.reshape(chans, -1)
        grad_two = weight_grad(cot_flat, grid_hidden, second_rate, DMAX, rows)
        bias_two_grad = lax.optimization_barrier(jnp.sum(cot_flat.astype(jnp.float32), 1))
        back_hidden = convolve(grid_of(cycle_pad(cot), DMAX), flipped, second_rate, DMAX, rows)
        sigm = jax.nn.sigmoid(pre_one)
        back_pre = (back_hidden * sigm * (1.0 + pre_one * (1.0 - sigm))).astype(jnp.bfloat16)
        grad_one = weight_grad(back_pre, grid_in, first_rate, DMAX, rows)
        bias_one_grad = lax.optimization_barrier(jnp.sum(back_pre.astype(jnp.float32), 1))
        return (output.reshape(chans, rows, -1), grad_one, bias_one_grad, grad_two, bias_two_grad)
    outputs, grad_one, bias_one_grad, grad_two, bias_two_grad = lax.map(one_sample, (inputs, cotangent))
    factor = 1.0 / math.sqrt(SAMPLES * WRAP * NS)
    return (outputs, lax.optimization_barrier(jnp.sum(grad_one, 0)) * factor, lax.optimization_barrier(jnp.sum(bias_one_grad, 0)) * factor, lax.optimization_barrier(jnp.sum(grad_two, 0)) * factor, lax.optimization_barrier(jnp.sum(bias_two_grad, 0)) * factor)
```

```python
import math

import jax
import jax.numpy as jnp
from jax import lax
from jax.experimental import pallas as pl
from jax.experimental.pallas import tpu as pltpu
from jax.sharding import Mesh
from jax.sharding import PartitionSpec as P

DMAX = 4
NR = 16
S = 16
NS = NR * S
CH = 64
BF = jnp.bfloat16
F32 = jnp.float32

VM = pl.BlockSpec(memory_space=pltpu.VMEM)
SM = pl.BlockSpec(memory_space=pltpu.SMEM)


def sds(shape, dtype):
    return jax.ShapeDtypeStruct(shape, dtype)


def call(kernel, outs, scratch=(), ins=None, flops=0, nbytes=0, name=None):
    return pl.pallas_call(
        kernel,
        out_shape=outs,
        in_specs=ins,
        out_specs=jax.tree.map(lambda _: VM, outs),
        scratch_shapes=list(scratch),
        cost_estimate=pl.CostEstimate(flops=flops, bytes_accessed=nbytes, transcendentals=0),
        compiler_params=pltpu.CompilerParams(vmem_limit_bytes=60 * 1024 * 1024),
        name=name,
    )


def nt(a, b):
    return lax.dot_general(a, b, (((1,), (1,)), ((), ())), preferred_element_type=F32)


def mm(a, b):
    return jnp.dot(a, b, preferred_element_type=F32)


def shift_matrix(tap, rate):
    dn = tap // 3 - 1
    ds = tap % 3 - 1
    src = lax.broadcasted_iota(jnp.int32, (NS, NS), 0)
    dst = lax.broadcasted_iota(jnp.int32, (NS, NS), 1)
    span = (dst & (S - 1)) + ds * rate
    hit = (src - dst == (dn * S + ds) * rate) & (span >= 0) & (span < S)
    return jnp.where(hit, 1.0, 0.0).astype(BF)


def swap_rows(x, major, minor):
    size = major * minor
    dst = lax.broadcasted_iota(jnp.int32, (size, size), 0)
    src = lax.broadcasted_iota(jnp.int32, (size, size), 1)
    want = (dst % major) * minor + dst // major
    perm = jnp.where(src == want, 1.0, 0.0).astype(BF)
    return mm(perm, x).astype(BF)


def shifted(x, rate, stack_ref):
    rows = x.shape[0] // CH

    def one(tap, carry):
        moved = mm(x, shift_matrix(tap, rate)).astype(BF)
        at = pl.ds(pl.multiple_of(tap * CH, CH), CH)
        for w in range(rows):
            stack_ref[at, w * NS : (w + 1) * NS] = moved[w * CH : (w + 1) * CH]
        return carry

    lax.fori_loop(0, 9, one, 0, unroll=True)


def lanes(row, count):
    return pl.ds(pl.multiple_of(row * NS, NS), count * NS)


def prep_kernel(rows, x_ref, c_ref, xp_ref, cp_ref, top_ref, bottom_ref):
    half = DMAX * CH
    for k, (src, dst) in enumerate(((x_ref, xp_ref), (c_ref, cp_ref))):
        swapped = swap_rows(src[...], CH, rows)
        dst[...] = swapped
        top_ref[k * half : (k + 1) * half] = swapped[:half]
        bottom_ref[k * half : (k + 1) * half] = swapped[rows * CH - half :]


def local_part(rows, x_ref, rate, w_ref, stack_ref, part_ref, pad_ref):
    shifted(x_ref[...], rate, stack_ref)
    pad_ref[...] = jnp.zeros_like(pad_ref)
    z = mm(w_ref[...], stack_ref[...])
    pad_ref[:, lanes(DMAX + rate, rows)] += z[:CH]
    pad_ref[:, lanes(DMAX, rows)] += z[CH : 2 * CH]
    pad_ref[:, lanes(DMAX - rate, rows)] += z[2 * CH :]
    part_ref[...] = pad_ref[:, DMAX * NS : (DMAX + rows) * NS]


def local_kernel(rows, d_ref, xp_ref, cp_ref, w1_ref, wf_ref, xs_ref, cs_ref, pre_ref, back_ref, pad_ref):
    local_part(rows, xp_ref, d_ref[0], w1_ref, xs_ref, pre_ref, pad_ref)
    local_part(rows, cp_ref, d_ref[1], wf_ref, cs_ref, back_ref, pad_ref)


def halo_part(rows, before, after, rate, w_ref, stack_ref, part, pad_ref):
    shifted(jnp.concatenate([before, after], 0), rate, stack_ref)
    pad_ref[:, DMAX * NS : (DMAX + rows) * NS] = part
    near = DMAX * NS
    pad_ref[:, lanes(rate, DMAX)] += mm(w_ref[:CH], stack_ref[:, :near])
    pad_ref[:, lanes(DMAX + rows - rate, DMAX)] += mm(w_ref[2 * CH :], stack_ref[:, near:])
    return pad_ref[:, DMAX * NS : (DMAX + rows) * NS]


def triple(rows, value, rate, pad_ref, out_ref):
    ext = rows + 2 * DMAX
    pad_ref[...] = jnp.zeros_like(pad_ref)
    pad_ref[:, 2 * DMAX * NS : (2 * DMAX + rows) * NS] = value
    for w in range(3):
        out_ref[w * CH : (w + 1) * CH] = pad_ref[:, lanes(DMAX + (1 - w) * rate, ext)]


def grad_kernel(
    rows, total, factor,
    d_ref, core_ref, b1_ref, up_ref, down_ref, w1_ref, wf_ref, xs_ref, cs_ref, pre_ref, back_ref, cp_ref,
    hid_ref, keep_ref, send_ref,
    pad_ref, pad16_ref, tri_ref, xh_ref, ch_ref, all_ref,
):
    r1 = d_ref[0]
    r2 = d_ref[1]
    half = DMAX * CH
    near = DMAX * NS
    mid = slice(near, near + rows * NS)
    far = slice(near + rows * NS, 2 * near + rows * NS)
    up = up_ref[...]
    down = down_ref[...]
    pre = halo_part(rows, up[:half], down[:half], r1, w1_ref, xh_ref, pre_ref[...], pad_ref) + b1_ref[...]
    sigm = 1.0 / (1.0 + jnp.exp(-pre))
    hidden = (pre * sigm).astype(BF)
    for w in range(rows):
        hid_ref[w * CH : (w + 1) * CH] = hidden[:, w * NS : (w + 1) * NS]
    slope = sigm * (1.0 + pre * (1.0 - sigm))
    back = halo_part(rows, up[half:], down[half:], r2, wf_ref, ch_ref, back_ref[...], pad_ref)
    back_pre = (back * slope).astype(BF)

    triple(rows, hidden, r2, pad16_ref, tri_ref)
    g2 = nt(cs_ref[...], tri_ref[:, mid])
    g2a = nt(ch_ref[:, :near], tri_ref[:CH, :near])
    g2b = nt(ch_ref[:, near:], tri_ref[2 * CH :, far])
    all_ref[:576] = jnp.concatenate([g2[:, :CH] + g2a, g2[:, CH : 2 * CH]], 1) * factor
    left2 = (g2[:, 2 * CH :] + g2b) * factor

    triple(rows, back_pre, r1, pad16_ref, tri_ref)
    g1 = nt(tri_ref[:, mid], xs_ref[...])
    g1a = nt(tri_ref[:CH, :near], xh_ref[:, :near])
    g1b = nt(tri_ref[2 * CH :, far], xh_ref[:, near:])
    g1 = jnp.concatenate([g1[:CH] + g1a, g1[CH : 2 * CH], g1[2 * CH :] + g1b], 0) * factor
    for k in range(4):
        all_ref[576 + 192 * k : 768 + 192 * k] = g1[:, 128 * k : 128 * (k + 1)]
    right = jnp.concatenate([left2[384:], g1[:, 512:]], 0)
    all_ref[1344:1728] = jnp.concatenate([left2[:384], right], 1)
    sum_one = jnp.sum(back_pre.astype(F32), 1, keepdims=True) * factor
    sum_two = jnp.zeros((CH, 1), F32)
    for w in range(rows):
        sum_two += jnp.sum(cp_ref[w * CH : (w + 1) * CH].astype(F32), 1, keepdims=True)
    col = lax.broadcasted_iota(jnp.int32, (CH, 128), 1)
    all_ref[1728:1792] = jnp.where(col < 64, sum_one, sum_two * factor)
    if total > 1792:
        all_ref[1792:] = jnp.zeros((total - 1792, 128), F32)
    core = core_ref[0]
    side = total // 2
    keep_ref[...] = all_ref[pl.ds(pl.multiple_of(core * side, 8), side)]
    send_ref[...] = all_ref[pl.ds(pl.multiple_of((1 - core) * side, 8), side)].astype(BF)


def pair_kernel(keep_ref, got_ref, out_ref):
    out_ref[...] = (keep_ref[...] + got_ref[...].astype(F32)).astype(BF)


def reduce_kernel(parts, got_ref, out_ref):
    total = got_ref[0].astype(F32)
    for k in range(1, parts):
        total = total + got_ref[k].astype(F32)
    total = total.astype(BF)
    for k in range(parts):
        out_ref[k] = total


def unpack_kernel(total, core_ref, mine_ref, other_ref, g1_ref, b1_ref, g2_ref, b2_ref, all_ref):
    core = core_ref[0]
    side = total // 2
    all_ref[pl.ds(pl.multiple_of(core * side, 8), side)] = mine_ref[...].astype(F32)
    all_ref[pl.ds(pl.multiple_of((1 - core) * side, 8), side)] = other_ref[...].astype(F32)
    corner = all_ref[1344:1728]
    for w in range(3):
        for ns in range(9):
            t = (2 - w) * 9 + 8 - ns
            if w < 2:
                block = all_ref[ns * CH : (ns + 1) * CH, w * CH : (w + 1) * CH]
            elif ns < 6:
                block = corner[ns * CH : (ns + 1) * CH, :CH]
            else:
                block = corner[(ns - 6) * CH : (ns - 5) * CH, CH:]
            g2_ref[:, t * CH : (t + 1) * CH] = block
    for w in range(3):
        for k in range(4):
            block = all_ref[576 + 192 * k + w * CH : 576 + 192 * k + (w + 1) * CH]
            g1_ref[:, w * 576 + k * 128 : w * 576 + (k + 1) * 128] = block
        g1_ref[:, w * 576 + 512 : (w + 1) * 576] = corner[192 + w * CH : 192 + (w + 1) * CH, CH:]
    b1_ref[...] = all_ref[1728:1792, :1]
    b2_ref[...] = all_ref[1728:1792, 64:65]


def predict_kernel(rows, d_ref, hid_ref, up_ref, down_ref, w2_ref, b2_ref, out_ref, stack_ref, halo_ref, pad_ref, mid_ref, row_ref):
    rate = d_ref[1]
    local_part(rows, hid_ref, rate, w2_ref, stack_ref, mid_ref, pad_ref)
    pred = halo_part(rows, up_ref[...], down_ref[...], rate, w2_ref, halo_ref, mid_ref[...], pad_ref)
    pred = (pred + b2_ref[...]).astype(BF)
    for w in range(rows):
        row_ref[w * CH : (w + 1) * CH] = pred[:, w * NS : (w + 1) * NS]
    out_ref[...] = swap_rows(row_ref[...], rows, CH)


def by_row_tap(weight):
    return weight.reshape(CH, 3, 576).transpose(1, 0, 2).reshape(192, 576)


def body(inputs, cotangent, weight_one, bias_one, weight_two, bias_two, dilation):
    rows = inputs.shape[2]
    wrap = lax.axis_size("wrap")
    pairs = lax.axis_size("x")
    group = wrap * pairs
    factor = 1.0 / math.sqrt(inputs.shape[0] * pairs * 2 * rows * wrap * NS)
    piece = -(-1792 // (2 * group) // 8) * 8 if 1792 % (16 * group) else 1792 // (2 * group)
    piece = max(8, -(-(-(-1792 // (2 * group))) // 8) * 8)
    total = 2 * group * piece
    cells = rows * NS
    up = [(i, (i + 1) % wrap) for i in range(wrap)]
    down = [(j, i) for i, j in up]
    swap = [(0, 1), (1, 0)]
    core = lax.axis_index("core").astype(jnp.int32).reshape(1)
    half = DMAX * CH

    x2 = inputs.reshape(CH * rows, NS)
    c2 = cotangent.reshape(CH * rows, NS)
    flat = sds((rows * CH, NS), BF)
    xp, cp, top, bottom = call(
        lambda *refs: prep_kernel(rows, *refs),
        (flat, flat, sds((2 * half, NS), BF), sds((2 * half, NS), BF)),
        ins=[VM, VM],
        name="prep",
    )(x2, c2)
    from_up = lax.ppermute(bottom, "wrap", up)
    from_down = lax.ppermute(top, "wrap", down)

    w1 = by_row_tap(weight_one)
    w2 = by_row_tap(weight_two)
    flip = jnp.transpose(weight_two.reshape(CH, 27, CH)[:, ::-1, :], (2, 1, 0)).reshape(CH, 27 * CH)
    wf = by_row_tap(flip)

    stack = sds((576, cells), BF)
    part = sds((CH, cells), F32)
    ext = (rows + 2 * DMAX) * NS
    xs, cs, pre, back = call(
        lambda *refs: local_kernel(rows, *refs),
        (stack, stack, part, part),
        scratch=[pltpu.VMEM((CH, ext), F32)],
        ins=[SM] + [VM] * 4,
        flops=4 * 10**9,
        nbytes=8 * 10**6,
        name="local",
    )(dilation, xp, cp, w1, wf)

    side = total // 2
    hid, keep, send = call(
        lambda *refs: grad_kernel(rows, total, factor, *refs),
        (flat, sds((side, 128), F32), sds((side, 128), BF)),
        scratch=[
            pltpu.VMEM((CH, ext), F32),
            pltpu.VMEM((CH, (rows + 4 * DMAX) * NS), BF),
            pltpu.VMEM((192, ext), BF),
            pltpu.VMEM((576, 2 * DMAX * NS), BF),
            pltpu.VMEM((576, 2 * DMAX * NS), BF),
            pltpu.VMEM((total, 128), F32),
        ],
        ins=[SM, SM] + [VM] * 10,
        flops=4 * 10**9,
        nbytes=8 * 10**6,
        name="grads",
    )(dilation, core, bias_one.reshape(CH, 1), from_up, from_down, w1, wf, xs, cs, pre, back, cp)

    got = lax.ppermute(send, "core", swap)
    hid_up = lax.ppermute(hid[rows * CH - half :], "wrap", up)
    hid_down = lax.ppermute(hid[:half], "wrap", down)
    both = call(pair_kernel, sds((side, 128), BF), ins=[VM, VM], name="pair")(keep, got)
    parts = lax.all_to_all(both.reshape(group, piece, 128), ("wrap", "x"), 0, 0, tiled=True)
    mine = call(
        lambda *refs: reduce_kernel(group, *refs),
        sds((group, piece, 128), BF),
        ins=[VM],
        name="reduce",
    )(parts)
    gathered = lax.all_to_all(mine, ("wrap", "x"), 0, 0, tiled=True).reshape(side, 128)
    other = lax.ppermute(gathered, "core", swap)
    g1, b1, g2, b2 = call(
        lambda *refs: unpack_kernel(total, *refs),
        (sds((CH, 1728), F32), sds((CH, 1), F32), sds((CH, 1728), F32), sds((CH, 1), F32)),
        scratch=[pltpu.VMEM((total, 128), F32)],
        ins=[SM, VM, VM],
        name="unpack",
    )(core, gathered, other)

    pred = call(
        lambda *refs: predict_kernel(rows, *refs),
        flat,
        scratch=[
            pltpu.VMEM((576, cells), BF),
            pltpu.VMEM((576, 2 * DMAX * NS), BF),
            pltpu.VMEM((CH, ext), F32),
            pltpu.VMEM((CH, cells), F32),
            pltpu.VMEM((rows * CH, NS), BF),
        ],
        ins=[SM] + [VM] * 5,
        flops=4 * 10**9,
        nbytes=10**6,
        name="predict",
    )(dilation, hid, hid_up, hid_down, w2, bias_two.reshape(CH, 1))
    return (
        pred.reshape(1, CH, rows, NS),
        g1,
        b1.reshape(CH),
        g2,
        b2.reshape(CH),
    )


def solution(mesh):
    wrap, samp = mesh.devices.shape
    split = Mesh(mesh.devices.reshape(wrap, samp // 2, 2), ("wrap", "x", "core"))
    field = P(("x", "core"), None, "wrap", None)
    return jax.shard_map(
        body,
        mesh=split,
        in_specs=(field, field, P(), P(), P(), P(), P()),
        out_specs=(field, P(), P(), P(), P()),
        check_vma=False,
    )
```

```python
import math

import jax
import jax.numpy as jnp
from jax import lax
from jax.experimental import pallas as pl
from jax.experimental.pallas import tpu as pltpu
from jax.sharding import Mesh
from jax.sharding import PartitionSpec as P

DMAX = 4
NR = 16
S = 16
NS = NR * S
CH = 64
TAPS = 9 * CH
HALF = DMAX * CH
NEAR = DMAX * NS
BF = jnp.bfloat16
F32 = jnp.float32

VM = pl.BlockSpec(memory_space=pltpu.VMEM)
SM = pl.BlockSpec(memory_space=pltpu.SMEM)
ANY = pl.BlockSpec(memory_space=pl.ANY)


def sds(shape, dtype):
    return jax.ShapeDtypeStruct(shape, dtype)


def call(kernel, outs, scratch=(), ins=None, flops=10**8, nbytes=10**6, name=None, mib=24):
    return pl.pallas_call(
        kernel,
        out_shape=outs,
        in_specs=ins,
        out_specs=jax.tree.map(lambda _: VM, outs),
        scratch_shapes=list(scratch),
        cost_estimate=pl.CostEstimate(flops=flops, bytes_accessed=nbytes, transcendentals=0),
        compiler_params=pltpu.CompilerParams(vmem_limit_bytes=mib * 1024 * 1024),
        name=name,
    )


def nt(a, b):
    return lax.dot_general(a, b, (((1,), (1,)), ((), ())), preferred_element_type=F32)


def mm(a, b):
    return jnp.dot(a, b, preferred_element_type=F32)


def select_matrix(rows, cols, target):
    src = lax.broadcasted_iota(jnp.int32, (rows, cols), 0)
    return jnp.where(src == target, 1.0, 0.0).astype(BF)


def shift_matrices(rate, out_ref):
    dst = lax.broadcasted_iota(jnp.int32, (1, NS), 1)
    for tap in range(9):
        dn = tap // 3 - 1
        ds = tap % 3 - 1
        span = (dst & (S - 1)) + ds * rate
        target = jnp.where((span >= 0) & (span < S), dst + (dn * S + ds) * rate, -1)
        out_ref[tap * NS : (tap + 1) * NS] = select_matrix(NS, NS, target)


def row_swap_matrix(major, minor):
    size = major * minor
    dst = lax.broadcasted_iota(jnp.int32, (size, 1), 0)
    want = (dst % major) * minor + dst // major
    src = lax.broadcasted_iota(jnp.int32, (size, size), 1)
    return jnp.where(src == want, 1.0, 0.0).astype(BF)


def shifted(x, mats_ref, stack_ref):
    rows = x.shape[0] // CH
    for tap in range(9):
        moved = x if tap == 4 else mm(x, mats_ref[tap * NS : (tap + 1) * NS]).astype(BF)
        for w in range(rows):
            stack_ref[tap * CH : (tap + 1) * CH, w * NS : (w + 1) * NS] = moved[w * CH : (w + 1) * CH]


def lanes(row, count):
    return pl.ds(pl.multiple_of(row * NS, NS), count * NS)


def column(row):
    i = lax.broadcasted_iota(jnp.int32, (CH, CH), 0)
    j = lax.broadcasted_iota(jnp.int32, (CH, CH), 1)
    return jnp.sum(jnp.where(i == j, jnp.broadcast_to(row, (CH, CH)), 0.0), 1, keepdims=True)


def prep_kernel(rows, par_ref, x_ref, c_ref, xp_ref, cp_ref, a_ref, b_ref):
    even = par_ref[0] == 0
    last = rows * CH - HALF
    first_at = pl.ds(pl.multiple_of(jnp.where(even, last, 0), CH), HALF)
    second_at = pl.ds(pl.multiple_of(jnp.where(even, 0, last), CH), HALF)
    perm = row_swap_matrix(CH, rows)
    for k, (src, dst) in enumerate(((x_ref, xp_ref), (c_ref, cp_ref))):
        dst[...] = mm(perm, src[...]).astype(BF)
        a_ref[k * HALF : (k + 1) * HALF] = dst[first_at]
        b_ref[k * HALF : (k + 1) * HALF] = dst[second_at]


def rows_by_tap(w_ref, out_ref):
    for w in range(3):
        out_ref[w * CH : (w + 1) * CH] = w_ref[:, w * TAPS : (w + 1) * TAPS]


def flipped_rows(w_ref, out_ref):
    turned = w_ref[...].astype(F32).T.astype(BF)
    for w in range(3):
        blocks = []
        for ns in range(9):
            t = (2 - w) * 9 + 8 - ns
            blocks.append(turned[t * CH : (t + 1) * CH])
        out_ref[w * CH : (w + 1) * CH] = jnp.concatenate(blocks, 1)


def local_part(rows, x, rate, w_ref, mats_ref, stack_ref, part_ref, pad_ref):
    shifted(x, mats_ref, stack_ref)
    pad_ref[:, :NEAR] = jnp.zeros((CH, NEAR), F32)
    pad_ref[:, NEAR + rows * NS :] = jnp.zeros((CH, NEAR), F32)
    z = mm(w_ref[...], stack_ref[...])
    pad_ref[:, NEAR : NEAR + rows * NS] = z[CH : 2 * CH]
    pad_ref[:, lanes(DMAX + rate, rows)] += z[:CH]
    pad_ref[:, lanes(DMAX - rate, rows)] += z[2 * CH :]
    part_ref[...] = pad_ref[:, NEAR : NEAR + rows * NS]


def local_kernel(
    rows,
    d_ref, xp_ref, cp_ref, one_ref, two_ref,
    xs_ref, cs_ref, pre_ref, back_ref, w1_ref, wf_ref, m1_ref, m2_ref,
    pad_ref,
):
    shift_matrices(d_ref[0], m1_ref)
    shift_matrices(d_ref[1], m2_ref)
    rows_by_tap(one_ref, w1_ref)
    flipped_rows(two_ref, wf_ref)
    local_part(rows, xp_ref[...], d_ref[0], w1_ref, m1_ref, xs_ref, pre_ref, pad_ref)
    local_part(rows, cp_ref[...], d_ref[1], wf_ref, m2_ref, cs_ref, back_ref, pad_ref)


def halo_part(rows, before, after, rate, w_ref, mats_ref, stack_ref, part, pad_ref):
    shifted(jnp.concatenate([before, after], 0), mats_ref, stack_ref)
    pad_ref[:, NEAR : NEAR + rows * NS] = part
    pad_ref[:, lanes(rate, DMAX)] += mm(w_ref[:CH], stack_ref[:, :NEAR])
    pad_ref[:, lanes(DMAX + rows - rate, DMAX)] += mm(w_ref[2 * CH :], stack_ref[:, NEAR:])
    return pad_ref[:, NEAR : NEAR + rows * NS]


def triple(rows, value, rate, pad_ref, out_ref):
    cells = rows * NS
    pad_ref[:, : 2 * NEAR] = jnp.zeros((CH, 2 * NEAR), BF)
    pad_ref[:, 2 * NEAR + cells :] = jnp.zeros((CH, 2 * NEAR), BF)
    pad_ref[:, 2 * NEAR : 2 * NEAR + cells] = value
    out_ref[:CH] = pad_ref[:, lanes(2 * DMAX + rate, rows)]
    out_ref[CH : 2 * CH] = value
    out_ref[2 * CH :] = pad_ref[:, lanes(2 * DMAX - rate, rows)]
    return pad_ref[:, lanes(DMAX + rate, DMAX)], pad_ref[:, lanes(2 * DMAX + rows - rate, DMAX)]


def grad_kernel(
    rows, total, factor,
    d_ref, core_ref, par_ref, b1_ref, a_ref, b_ref, w1_ref, wf_ref, xs_ref, cs_ref, pre_ref, back_ref, m1_ref, m2_ref,
    hid_ref, ha_ref, hb_ref, keep_ref, send_ref,
    pad_ref, pad16_ref, tri_ref, xh_ref, ch_ref, all_ref,
):
    r1 = d_ref[0]
    r2 = d_ref[1]
    even = par_ref[0] == 0
    cells = rows * NS
    one = a_ref[...]
    two = b_ref[...]
    up = jnp.where(even, two, one)
    down = jnp.where(even, one, two)
    pre = halo_part(rows, up[:HALF], down[:HALF], r1, w1_ref, m1_ref, xh_ref, pre_ref[...], pad_ref)
    pre = pre + column(b1_ref[...])
    sigm = 1.0 / (1.0 + jnp.exp(-pre))
    hidden = (pre * sigm).astype(BF)
    for w in range(rows):
        hid_ref[w * CH : (w + 1) * CH] = hidden[:, w * NS : (w + 1) * NS]
    last = rows * CH - HALF
    ha_ref[...] = hid_ref[pl.ds(pl.multiple_of(jnp.where(even, last, 0), CH), HALF)]
    hb_ref[...] = hid_ref[pl.ds(pl.multiple_of(jnp.where(even, 0, last), CH), HALF)]
    slope = sigm * (1.0 + pre * (1.0 - sigm))
    back = halo_part(rows, up[HALF:], down[HALF:], r2, wf_ref, m2_ref, ch_ref, back_ref[...], pad_ref)
    back_pre = (back * slope).astype(BF)

    before, after = triple(rows, hidden, r2, pad16_ref, tri_ref)
    g2 = nt(cs_ref[...], tri_ref[...])
    g2a = nt(ch_ref[:, :NEAR], before)
    g2b = nt(ch_ref[:, NEAR:], after)
    all_ref[:TAPS] = jnp.concatenate([g2[:, :CH] + g2a, g2[:, CH : 2 * CH]], 1) * factor
    left2 = (g2[:, 2 * CH :] + g2b) * factor

    before, after = triple(rows, back_pre, r1, pad16_ref, tri_ref)
    g1 = nt(tri_ref[...], xs_ref[...])
    g1a = nt(before, xh_ref[:, :NEAR])
    g1b = nt(after, xh_ref[:, NEAR:])
    g1 = jnp.concatenate([g1[:CH] + g1a, g1[CH : 2 * CH], g1[2 * CH :] + g1b], 0) * factor
    for k in range(4):
        all_ref[576 + 192 * k : 768 + 192 * k] = g1[:, 128 * k : 128 * (k + 1)]
    right = jnp.concatenate([left2[384:], g1[:, 512:]], 0)
    all_ref[1344:1728] = jnp.concatenate([left2[:384], right], 1)
    ones = jnp.ones((8, cells), BF)
    sums = jnp.concatenate([nt(ones, back_pre), nt(ones, cs_ref[4 * CH : 5 * CH])], 1)
    all_ref[1728:1736] = sums * factor
    all_ref[1736:] = jnp.zeros((total - 1736, 128), F32)
    core = core_ref[0]
    side = total // 2
    keep_ref[...] = all_ref[pl.ds(pl.multiple_of(core * side, 8), side)]
    send_ref[...] = all_ref[pl.ds(pl.multiple_of((1 - core) * side, 8), side)].astype(BF)


def pair_kernel(keep_ref, got_ref, out_ref):
    out_ref[...] = (keep_ref[...] + got_ref[...].astype(F32)).astype(BF)


def reduce_kernel(parts, got_ref, order_ref, out_ref):
    total = got_ref[0].astype(F32)
    for k in range(1, parts):
        total = total + got_ref[k].astype(F32)
    total = total.astype(BF)
    for k in range(parts):
        out_ref[k] = total


def unpack_kernel(total, core_ref, mine_ref, other_ref, g1_ref, b1_ref, g2_ref, b2_ref, all_ref):
    core = core_ref[0]
    side = total // 2
    all_ref[pl.ds(pl.multiple_of(core * side, 8), side)] = mine_ref[...].astype(F32)
    all_ref[pl.ds(pl.multiple_of((1 - core) * side, 8), side)] = other_ref[...].astype(F32)
    corner = all_ref[1344:1728]
    blocks = [None] * 27
    for w in range(3):
        for ns in range(9):
            if w < 2:
                block = all_ref[ns * CH : (ns + 1) * CH, w * CH : (w + 1) * CH]
            elif ns < 6:
                block = corner[ns * CH : (ns + 1) * CH, :CH]
            else:
                block = corner[(ns - 6) * CH : (ns - 5) * CH, CH:]
            blocks[(2 - w) * 9 + 8 - ns] = block
    g2_ref[...] = jnp.concatenate(blocks, 1)
    blocks = []
    for w in range(3):
        for k in range(4):
            blocks.append(all_ref[576 + 192 * k + w * CH : 576 + 192 * k + (w + 1) * CH])
        blocks.append(corner[192 + w * CH : 192 + (w + 1) * CH, CH:])
    g1_ref[...] = jnp.concatenate(blocks, 1)
    b1_ref[...] = all_ref[1728:1729, :CH]
    b2_ref[...] = all_ref[1728:1729, CH:]


def guess_kernel(rows, d_ref, hid_ref, two_ref, m2_ref, order_ref, part_ref, w2_ref, stack_ref, pad_ref):
    rows_by_tap(two_ref, w2_ref)
    local_part(rows, hid_ref[...], d_ref[1], w2_ref, m2_ref, stack_ref, part_ref, pad_ref)


def predict_kernel(
    rows, d_ref, par_ref, a_ref, b_ref, w2_ref, b2_ref, m2_ref, part_ref, out_ref, halo_ref, pad_ref, row_ref
):
    even = par_ref[0] == 0
    one = a_ref[...]
    two = b_ref[...]
    up = jnp.where(even, two, one)
    down = jnp.where(even, one, two)
    pred = halo_part(rows, up, down, d_ref[1], w2_ref, m2_ref, halo_ref, part_ref[...], pad_ref)
    pred = (pred + column(b2_ref[...])).astype(BF)
    for w in range(rows):
        row_ref[w * CH : (w + 1) * CH] = pred[:, w * NS : (w + 1) * NS]
    out_ref[...] = mm(row_swap_matrix(rows, CH), row_ref[...]).astype(BF)


def body(inputs, cotangent, weight_one, bias_one, weight_two, bias_two, dilation):
    rows = inputs.shape[2]
    wrap = lax.axis_size("wrap")
    pairs = lax.axis_size("x")
    group = wrap * pairs
    factor = 1.0 / math.sqrt(inputs.shape[0] * pairs * 2 * rows * wrap * NS)
    piece = -(-1737 // (2 * group * 8)) * 8
    total = 2 * group * piece
    side = total // 2
    cells = rows * NS
    ext = cells + 2 * NEAR
    first = [(i, i ^ 1) for i in range(wrap)]
    second = [(i, (i + 1) % wrap if i % 2 else (i - 1) % wrap) for i in range(wrap)]
    swap = [(0, 1), (1, 0)]
    core = lax.axis_index("core").astype(jnp.int32).reshape(1)
    parity = (lax.axis_index("wrap").astype(jnp.int32) & 1).reshape(1)

    x2 = inputs.reshape(CH * rows, NS)
    c2 = cotangent.reshape(CH * rows, NS)
    flat = sds((rows * CH, NS), BF)
    halo = sds((2 * HALF, NS), BF)
    xp, cp, send_a, send_b = call(
        lambda *refs: prep_kernel(rows, *refs),
        (flat, flat, halo, halo),
        ins=[SM, VM, VM],
        name="prep",
        mib=8,
    )(parity, x2, c2)
    got_a = lax.ppermute(send_a, "wrap", first)
    got_b = lax.ppermute(send_b, "wrap", second)

    stack = sds((TAPS, cells), BF)
    part = sds((CH, cells), F32)
    wide = sds((3 * CH, TAPS), BF)
    mats = sds((9 * NS, NS), BF)
    xs, cs, pre, back, w1, wf, m1, m2 = call(
        lambda *refs: local_kernel(rows, *refs),
        (stack, stack, part, part, wide, wide, mats, mats),
        scratch=[pltpu.VMEM((CH, ext), F32)],
        ins=[SM] + [VM] * 4,
        flops=4 * 10**9,
        nbytes=8 * 10**6,
        name="local",
    )(dilation, xp, cp, weight_one, weight_two)

    edge = sds((HALF, NS), BF)
    hid, hid_a, hid_b, keep, send = call(
        lambda *refs: grad_kernel(rows, total, factor, *refs),
        (flat, edge, edge, sds((side, 128), F32), sds((side, 128), BF)),
        scratch=[
            pltpu.VMEM((CH, ext), F32),
            pltpu.VMEM((CH, cells + 4 * NEAR), BF),
            pltpu.VMEM((3 * CH, cells), BF),
            pltpu.VMEM((TAPS, 2 * NEAR), BF),
            pltpu.VMEM((TAPS, 2 * NEAR), BF),
            pltpu.VMEM((total, 128), F32),
        ],
        ins=[SM, SM, SM] + [VM] * 11,
        flops=4 * 10**9,
        nbytes=8 * 10**6,
        name="grads",
    )(dilation, core, parity, bias_one.reshape(1, CH), got_a, got_b, w1, wf, xs, cs, pre, back, m1, m2)

    got = lax.ppermute(send, "core", swap)
    both = call(pair_kernel, sds((side, 128), BF), ins=[VM, VM], name="pair", mib=8)(keep, got)
    hid_a, hid_b, both = lax.optimization_barrier((hid_a, hid_b, both))
    with jax.named_scope("scatter"):
        parts = lax.all_to_all(both.reshape(group, piece, 128), ("wrap", "x"), 0, 0, tiled=True)
    halo_a = lax.ppermute(hid_a, "wrap", first)
    halo_b = lax.ppermute(hid_b, "wrap", second)
    guess, w2 = call(
        lambda *refs: guess_kernel(rows, *refs),
        (part, wide),
        scratch=[pltpu.VMEM((TAPS, cells), BF), pltpu.VMEM((CH, ext), F32)],
        ins=[SM, VM, VM, VM, ANY],
        flops=4 * 10**9,
        nbytes=8 * 10**6,
        name="guess",
    )(dilation, hid, weight_two, m2, both)
    mine = call(
        lambda *refs: reduce_kernel(group, *refs),
        sds((group, piece, 128), BF),
        ins=[VM, ANY],
        name="reduce",
        mib=8,
    )(parts, guess)
    with jax.named_scope("gather"):
        gathered = lax.all_to_all(mine, ("wrap", "x"), 0, 0, tiled=True).reshape(side, 128)
    other = lax.ppermute(gathered, "core", swap)
    pred = call(
        lambda *refs: predict_kernel(rows, *refs),
        flat,
        scratch=[
            pltpu.VMEM((TAPS, 2 * NEAR), BF),
            pltpu.VMEM((CH, ext), F32),
            pltpu.VMEM((rows * CH, NS), BF),
        ],
        ins=[SM, SM] + [VM] * 6,
        flops=4 * 10**9,
        nbytes=8 * 10**6,
        name="predict",
    )(dilation, parity, halo_a, halo_b, w2, bias_two.reshape(1, CH), m2, guess)
    row = sds((1, CH), F32)
    full = sds((CH, 3 * TAPS), F32)
    g1, b1, g2, b2 = call(
        lambda *refs: unpack_kernel(total, *refs),
        (full, row, full, row),
        scratch=[pltpu.VMEM((total, 128), F32)],
        ins=[SM, VM, VM],
        name="unpack",
        mib=8,
    )(core, gathered, other)
    return (pred.reshape(1, CH, rows, NS), g1, b1.reshape(CH), g2, b2.reshape(CH))


def solution(mesh):
    wrap, samp = mesh.devices.shape
    split = Mesh(mesh.devices.reshape(wrap, samp // 2, 2), ("wrap", "x", "core"))
    field = P(("x", "core"), None, "wrap", None)
    return jax.shard_map(
        body,
        mesh=split,
        in_specs=(field, field, P(), P(), P(), P(), P()),
        out_specs=(field, P(), P(), P(), P()),
        check_vma=False,
    )
```

```python
import math

import jax
import jax.numpy as jnp
from jax import lax
from jax.experimental import pallas as pl
from jax.experimental.pallas import tpu as pltpu
from jax.sharding import Mesh
from jax.sharding import PartitionSpec as P


DMAX = 4
NR = 16
S = 16
NS = NR * S
CH = 64
TAPS = 9 * CH
HALF = DMAX * CH
NEAR = DMAX * NS
BF = jnp.bfloat16
F32 = jnp.float32

VM = pl.BlockSpec(memory_space=pltpu.VMEM)
SM = pl.BlockSpec(memory_space=pltpu.SMEM)
HBM = pl.BlockSpec(memory_space=pltpu.HBM)


def sds(shape, dtype):
    return jax.ShapeDtypeStruct(shape, dtype)


def call(kernel, outs, scratch=(), ins=None, flops=10**8, nbytes=10**6, mib=16):
    return pl.pallas_call(
        kernel,
        out_shape=outs,
        in_specs=ins,
        out_specs=jax.tree.map(lambda _: VM, outs),
        scratch_shapes=list(scratch),
        cost_estimate=pl.CostEstimate(flops=flops, bytes_accessed=nbytes, transcendentals=0),
        compiler_params=pltpu.CompilerParams(vmem_limit_bytes=mib * 1024 * 1024),
    )


def nt(a, b):
    return lax.dot_general(a, b, (((1,), (1,)), ((), ())), preferred_element_type=F32)


def mm(a, b):
    return jnp.dot(a, b, preferred_element_type=F32)


def select_matrix(rows, cols, target):
    src = lax.broadcasted_iota(jnp.int32, (rows, cols), 0)
    return jnp.where(src == target, 1.0, 0.0).astype(BF)


def shift_matrices(rate, out_ref):
    dst = lax.broadcasted_iota(jnp.int32, (1, NS), 1)
    for tap in range(9):
        dn = tap // 3 - 1
        ds = tap % 3 - 1
        span = (dst & (S - 1)) + ds * rate
        target = jnp.where((span >= 0) & (span < S), dst + (dn * S + ds) * rate, -1)
        out_ref[tap * NS : (tap + 1) * NS] = select_matrix(NS, NS, target)


def row_swap_matrix(major, minor):
    size = major * minor
    dst = lax.broadcasted_iota(jnp.int32, (size, 1), 0)
    want = (dst % major) * minor + dst // major
    src = lax.broadcasted_iota(jnp.int32, (size, size), 1)
    return jnp.where(src == want, 1.0, 0.0).astype(BF)


def shifted(x, mats_ref, stack_ref):
    rows = x.shape[0] // CH
    for tap in range(9):
        moved = x if tap == 4 else mm(x, mats_ref[tap * NS : (tap + 1) * NS]).astype(BF)
        for w in range(rows):
            stack_ref[tap * CH : (tap + 1) * CH, w * NS : (w + 1) * NS] = moved[w * CH : (w + 1) * CH]


def lanes(row, count):
    return pl.ds(pl.multiple_of(row * NS, NS), count * NS)


def column(row):
    i = lax.broadcasted_iota(jnp.int32, (CH, CH), 0)
    j = lax.broadcasted_iota(jnp.int32, (CH, CH), 1)
    return jnp.sum(jnp.where(i == j, jnp.broadcast_to(row, (CH, CH)), 0.0), 1, keepdims=True)


def prep_kernel(rows, par_ref, core_ref, x_hbm, c_hbm, xp_ref, cp_ref, a_ref, b_ref, x_ref, c_ref, sem):
    copies = [pltpu.make_async_copy(x_hbm, x_ref, sem.at[0]), pltpu.make_async_copy(c_hbm, c_ref, sem.at[1])]
    for copy in copies:
        copy.start()
    even = par_ref[0] == 0
    last = rows * CH - HALF
    first_at = pl.ds(pl.multiple_of(jnp.where(even, last, 0), CH), HALF)
    second_at = pl.ds(pl.multiple_of(jnp.where(even, 0, last), CH), HALF)
    perm = row_swap_matrix(CH, rows)
    for k, (src, dst) in enumerate(((x_ref, xp_ref), (c_ref, cp_ref))):
        copies[k].wait()
        dst[...] = mm(perm, src[...]).astype(BF)
        a_ref[k * HALF : (k + 1) * HALF] = dst[first_at]
        b_ref[k * HALF : (k + 1) * HALF] = dst[second_at]


def rows_by_tap(w_ref, out_ref):
    for w in range(3):
        out_ref[w * CH : (w + 1) * CH] = w_ref[:, w * TAPS : (w + 1) * TAPS]


def flipped_rows(w_ref, out_ref):
    turned = w_ref[...].astype(F32).T.astype(BF)
    for w in range(3):
        blocks = []
        for ns in range(9):
            t = (2 - w) * 9 + 8 - ns
            blocks.append(turned[t * CH : (t + 1) * CH])
        out_ref[w * CH : (w + 1) * CH] = jnp.concatenate(blocks, 1)


def local_part(rows, x, rate, w_ref, mats_ref, stack_ref, part_ref, pad_ref):
    shifted(x, mats_ref, stack_ref)
    pad_ref[:, :NEAR] = jnp.zeros((CH, NEAR), F32)
    pad_ref[:, NEAR + rows * NS :] = jnp.zeros((CH, NEAR), F32)
    z = mm(w_ref[...], stack_ref[...])
    pad_ref[:, NEAR : NEAR + rows * NS] = z[CH : 2 * CH]
    pad_ref[:, lanes(DMAX + rate, rows)] += z[:CH]
    pad_ref[:, lanes(DMAX - rate, rows)] += z[2 * CH :]
    part_ref[...] = pad_ref[:, NEAR : NEAR + rows * NS]


def local_kernel(
    rows,
    d_ref, xp_ref, cp_ref, one_hbm, two_hbm,
    xs_ref, cs_ref, pre_ref, back_ref, w1_ref, wf_ref, m1_ref, m2_ref,
    pad_ref, one_ref, two_ref, sem,
):
    copies = [pltpu.make_async_copy(one_hbm, one_ref, sem.at[0]), pltpu.make_async_copy(two_hbm, two_ref, sem.at[1])]
    for copy in copies:
        copy.start()
    shift_matrices(d_ref[0], m1_ref)
    shift_matrices(d_ref[1], m2_ref)
    copies[0].wait()
    rows_by_tap(one_ref, w1_ref)
    local_part(rows, xp_ref[...], d_ref[0], w1_ref, m1_ref, xs_ref, pre_ref, pad_ref)
    copies[1].wait()
    flipped_rows(two_ref, wf_ref)
    local_part(rows, cp_ref[...], d_ref[1], wf_ref, m2_ref, cs_ref, back_ref, pad_ref)


def side_part(rows, before, cells, rate, w_ref, mats_ref, stack_ref, part, pad_ref):
    shifted(cells, mats_ref, stack_ref)
    pad_ref[:, NEAR : NEAR + rows * NS] = part
    weight = w_ref[pl.ds(pl.multiple_of(jnp.where(before, 0, 2 * CH), CH), CH)]
    pad_ref[:, lanes(jnp.where(before, rate, DMAX + rows - rate), DMAX)] += mm(weight, stack_ref[...])
    return pad_ref[:, NEAR : NEAR + rows * NS]


def near_kernel(
    rows,
    d_ref, par_ref, a_ref, w1_ref, wf_ref, m1_ref, m2_ref, pre_ref, back_ref,
    xa_ref, ca_ref, pre_out, back_out,
    pad_ref,
):
    before = par_ref[0] != 0
    pre_out[...] = side_part(
        rows, before, a_ref[:HALF], d_ref[0], w1_ref, m1_ref, xa_ref, pre_ref[...], pad_ref
    )
    back_out[...] = side_part(
        rows, before, a_ref[HALF:], d_ref[1], wf_ref, m2_ref, ca_ref, back_ref[...], pad_ref
    )


def halo_part(rows, before, after, rate, w_ref, mats_ref, stack_ref, part, pad_ref):
    shifted(jnp.concatenate([before, after], 0), mats_ref, stack_ref)
    pad_ref[:, NEAR : NEAR + rows * NS] = part
    pad_ref[:, lanes(rate, DMAX)] += mm(w_ref[:CH], stack_ref[:, :NEAR])
    pad_ref[:, lanes(DMAX + rows - rate, DMAX)] += mm(w_ref[2 * CH :], stack_ref[:, NEAR:])
    return pad_ref[:, NEAR : NEAR + rows * NS]


def triple(rows, value, rate, pad_ref, out_ref):
    cells = rows * NS
    pad_ref[:, : 2 * NEAR] = jnp.zeros((CH, 2 * NEAR), BF)
    pad_ref[:, 2 * NEAR + cells :] = jnp.zeros((CH, 2 * NEAR), BF)
    pad_ref[:, 2 * NEAR : 2 * NEAR + cells] = value
    out_ref[:CH] = pad_ref[:, lanes(2 * DMAX + rate, rows)]
    out_ref[CH : 2 * CH] = value
    out_ref[2 * CH :] = pad_ref[:, lanes(2 * DMAX - rate, rows)]
    def side(before):
        return pad_ref[:, lanes(jnp.where(before, DMAX + rate, 2 * DMAX + rows - rate), DMAX)]

    return side


def grad_kernel(
    rows, total, factor,
    d_ref, core_ref, par_ref, b1_ref, b_ref, w1_ref, wf_ref, xs_ref, cs_ref, xa_ref, ca_ref, pre_ref, back_ref,
    m1_ref, m2_ref,
    hid_ref, ha_ref, hb_ref, keep_ref, send_ref,
    pad_ref, pad16_ref, tri_ref, xb_ref, cb_ref, all_ref,
):
    r1 = d_ref[0]
    r2 = d_ref[1]
    even = par_ref[0] == 0
    odd = par_ref[0] != 0
    cells = rows * NS
    pre = side_part(rows, even, b_ref[:HALF], r1, w1_ref, m1_ref, xb_ref, pre_ref[...], pad_ref)
    pre = pre + column(b1_ref[...])
    sigm = 1.0 / (1.0 + jnp.exp(-pre))
    hidden = (pre * sigm).astype(BF)
    for w in range(rows):
        hid_ref[w * CH : (w + 1) * CH] = hidden[:, w * NS : (w + 1) * NS]
    last = rows * CH - HALF
    ha_ref[...] = hid_ref[pl.ds(pl.multiple_of(jnp.where(even, last, 0), CH), HALF)]
    hb_ref[...] = hid_ref[pl.ds(pl.multiple_of(jnp.where(even, 0, last), CH), HALF)]
    slope = sigm * (1.0 + pre * (1.0 - sigm))
    back = side_part(rows, even, b_ref[HALF:], r2, wf_ref, m2_ref, cb_ref, back_ref[...], pad_ref)
    back_pre = (back * slope).astype(BF)

    side = triple(rows, hidden, r2, pad16_ref, tri_ref)
    g2 = nt(cs_ref[...], tri_ref[...])
    g2a = nt(ca_ref[...], side(odd))
    g2b = nt(cb_ref[...], side(even))
    low = jnp.where(even, g2b, g2a)
    high = jnp.where(even, g2a, g2b)
    all_ref[:TAPS] = jnp.concatenate([g2[:, :CH] + low, g2[:, CH : 2 * CH]], 1) * factor
    left2 = (g2[:, 2 * CH :] + high) * factor

    side = triple(rows, back_pre, r1, pad16_ref, tri_ref)
    g1 = nt(tri_ref[...], xs_ref[...])
    g1a = nt(side(odd), xa_ref[...])
    g1b = nt(side(even), xb_ref[...])
    low = jnp.where(even, g1b, g1a)
    high = jnp.where(even, g1a, g1b)
    g1 = jnp.concatenate([g1[:CH] + low, g1[CH : 2 * CH], g1[2 * CH :] + high], 0) * factor
    for k in range(4):
        all_ref[576 + 192 * k : 768 + 192 * k] = g1[:, 128 * k : 128 * (k + 1)]
    right = jnp.concatenate([left2[384:], g1[:, 512:]], 0)
    all_ref[1344:1728] = jnp.concatenate([left2[:384], right], 1)
    ones = jnp.ones((8, cells), BF)
    sums = jnp.concatenate([nt(ones, back_pre), nt(ones, cs_ref[4 * CH : 5 * CH])], 1)
    all_ref[1728:1736] = sums * factor
    all_ref[1736:] = jnp.zeros((total - 1736, 128), F32)
    core = core_ref[0]
    side = total // 2
    keep_ref[...] = all_ref[pl.ds(pl.multiple_of(core * side, 8), side)]
    send_ref[...] = all_ref[pl.ds(pl.multiple_of((1 - core) * side, 8), side)].astype(BF)


def pair_kernel(keep_ref, got_ref, out_ref):
    out_ref[...] = (keep_ref[...] + got_ref[...].astype(F32)).astype(BF)


def reduce_kernel(parts, got_ref, out_ref):
    total = got_ref[0].astype(F32)
    for k in range(1, parts):
        total = total + got_ref[k].astype(F32)
    total = total.astype(BF)
    for k in range(parts):
        out_ref[k] = total


def unpack_kernel(total, core_ref, mine_ref, other_ref, g1_ref, b1_ref, g2_ref, b2_ref, all_ref):
    core = core_ref[0]
    side = total // 2
    all_ref[pl.ds(pl.multiple_of(core * side, 8), side)] = mine_ref[...].astype(F32)
    all_ref[pl.ds(pl.multiple_of((1 - core) * side, 8), side)] = other_ref[...].astype(F32)
    corner = all_ref[1344:1728]
    blocks = [None] * 27
    for w in range(3):
        for ns in range(9):
            if w < 2:
                block = all_ref[ns * CH : (ns + 1) * CH, w * CH : (w + 1) * CH]
            elif ns < 6:
                block = corner[ns * CH : (ns + 1) * CH, :CH]
            else:
                block = corner[(ns - 6) * CH : (ns - 5) * CH, CH:]
            blocks[(2 - w) * 9 + 8 - ns] = block
    g2_ref[...] = jnp.concatenate(blocks, 1)
    blocks = []
    for w in range(3):
        for k in range(4):
            blocks.append(all_ref[576 + 192 * k + w * CH : 576 + 192 * k + (w + 1) * CH])
        blocks.append(corner[192 + w * CH : 192 + (w + 1) * CH, CH:])
    g1_ref[...] = jnp.concatenate(blocks, 1)
    b1_ref[...] = all_ref[1728:1729, :CH]
    b2_ref[...] = all_ref[1728:1729, CH:]


def guess_kernel(rows, d_ref, hid_ref, two_hbm, m2_ref, part_ref, w2_ref, stack_ref, pad_ref, two_ref, sem):
    copy = pltpu.make_async_copy(two_hbm, two_ref, sem)
    copy.start()
    copy.wait()
    rows_by_tap(two_ref, w2_ref)
    local_part(rows, hid_ref[...], d_ref[1], w2_ref, m2_ref, stack_ref, part_ref, pad_ref)


def predict_kernel(
    rows, d_ref, par_ref, a_ref, b_ref, w2_ref, b2_ref, m2_ref, part_ref, out_ref, halo_ref, pad_ref, row_ref
):
    even = par_ref[0] == 0
    one = a_ref[...]
    two = b_ref[...]
    up = jnp.where(even, two, one)
    down = jnp.where(even, one, two)
    pred = halo_part(rows, up, down, d_ref[1], w2_ref, m2_ref, halo_ref, part_ref[...], pad_ref)
    pred = (pred + column(b2_ref[...])).astype(BF)
    for w in range(rows):
        row_ref[w * CH : (w + 1) * CH] = pred[:, w * NS : (w + 1) * NS]
    out_ref[...] = mm(row_swap_matrix(rows, CH), row_ref[...]).astype(BF)


def body(inputs, cotangent, weight_one, bias_one, weight_two, bias_two, dilation):
    rows = inputs.shape[2]
    wrap = lax.axis_size("wrap")
    pairs = lax.axis_size("x")
    group = wrap * pairs
    factor = 1.0 / math.sqrt(inputs.shape[0] * pairs * 2 * rows * wrap * NS)
    piece = -(-1737 // (2 * group * 8)) * 8
    total = 2 * group * piece
    side = total // 2
    cells = rows * NS
    ext = cells + 2 * NEAR
    first = [(i, i ^ 1) for i in range(wrap)]
    second = [(i, (i + 1) % wrap if i % 2 else (i - 1) % wrap) for i in range(wrap)]
    swap = [(0, 1), (1, 0)]
    core = lax.axis_index("core").astype(jnp.int32).reshape(1)
    parity = (lax.axis_index("wrap").astype(jnp.int32) & 1).reshape(1)

    x2 = inputs.reshape(CH * rows, NS)
    c2 = cotangent.reshape(CH * rows, NS)
    flat = sds((rows * CH, NS), BF)
    halo = sds((2 * HALF, NS), BF)
    xp, cp, send_a, send_b = call(
        lambda *refs: prep_kernel(rows, *refs),
        (flat, flat, halo, halo),
        scratch=[pltpu.VMEM((rows * CH, NS), BF), pltpu.VMEM((rows * CH, NS), BF), pltpu.SemaphoreType.DMA((2,))],
        ins=[SM, SM, HBM, HBM],
        mib=8,
    )(parity, core, x2, c2)
    got_a = lax.ppermute(send_a, "wrap", first)
    got_b = lax.ppermute(send_b, "wrap", second)

    stack = sds((TAPS, cells), BF)
    part = sds((CH, cells), F32)
    wide = sds((3 * CH, TAPS), BF)
    mats = sds((9 * NS, NS), BF)
    xs, cs, pre, back, w1, wf, m1, m2 = call(
        lambda *refs: local_kernel(rows, *refs),
        (stack, stack, part, part, wide, wide, mats, mats),
        scratch=[
            pltpu.VMEM((CH, ext), F32),
            pltpu.VMEM((CH, 3 * TAPS), BF),
            pltpu.VMEM((CH, 3 * TAPS), BF),
            pltpu.SemaphoreType.DMA((2,)),
        ],
        ins=[SM, VM, VM, HBM, HBM],
        flops=4 * 10**9,
        nbytes=8 * 10**6,
        mib=14,
    )(dilation, xp, cp, weight_one, weight_two)

    beside = sds((TAPS, NEAR), BF)
    xa, ca, pre, back = call(
        lambda *refs: near_kernel(rows, *refs),
        (beside, beside, part, part),
        scratch=[pltpu.VMEM((CH, ext), F32)],
        ins=[SM, SM] + [VM] * 7,
        flops=2 * 10**9,
        nbytes=4 * 10**6,
        mib=10,
    )(dilation, parity, got_a, w1, wf, m1, m2, pre, back)

    edge = sds((HALF, NS), BF)
    hid, hid_a, hid_b, keep, send = call(
        lambda *refs: grad_kernel(rows, total, factor, *refs),
        (flat, edge, edge, sds((side, 128), F32), sds((side, 128), BF)),
        scratch=[
            pltpu.VMEM((CH, ext), F32),
            pltpu.VMEM((CH, cells + 4 * NEAR), BF),
            pltpu.VMEM((3 * CH, cells), BF),
            pltpu.VMEM((TAPS, NEAR), BF),
            pltpu.VMEM((TAPS, NEAR), BF),
            pltpu.VMEM((total, 128), F32),
        ],
        ins=[SM, SM, SM] + [VM] * 12,
        flops=4 * 10**9,
        nbytes=8 * 10**6,
        mib=14,
    )(dilation, core, parity, bias_one.reshape(1, CH), got_b, w1, wf, xs, cs, xa, ca, pre, back, m1, m2)

    got = lax.ppermute(send, "core", swap)
    both = call(pair_kernel, sds((side, 128), BF), ins=[VM, VM], mib=8)(keep, got)
    parts = lax.all_to_all(both.reshape(group, piece, 128), ("wrap", "x"), 0, 0, tiled=True)
    halo_a = lax.ppermute(hid_a, "wrap", first)
    halo_b = lax.ppermute(hid_b, "wrap", second)
    guess, w2 = call(
        lambda *refs: guess_kernel(rows, *refs),
        (part, wide),
        scratch=[
            pltpu.VMEM((TAPS, cells), BF),
            pltpu.VMEM((CH, ext), F32),
            pltpu.VMEM((CH, 3 * TAPS), BF),
            pltpu.SemaphoreType.DMA,
        ],
        ins=[SM, VM, HBM, VM],
        flops=4 * 10**9,
        nbytes=8 * 10**6,
        mib=10,
    )(dilation, hid, weight_two, m2)
    mine = call(lambda *refs: reduce_kernel(group, *refs), sds((group, piece, 128), BF), ins=[VM], mib=8)(parts)
    gathered = lax.all_to_all(mine, ("wrap", "x"), 0, 0, tiled=True).reshape(side, 128)
    other = lax.ppermute(gathered, "core", swap)
    pred = call(
        lambda *refs: predict_kernel(rows, *refs),
        flat,
        scratch=[
            pltpu.VMEM((TAPS, 2 * NEAR), BF),
            pltpu.VMEM((CH, ext), F32),
            pltpu.VMEM((rows * CH, NS), BF),
        ],
        ins=[SM, SM] + [VM] * 6,
        flops=4 * 10**9,
        nbytes=8 * 10**6,
        mib=8,
    )(dilation, parity, halo_a, halo_b, w2, bias_two.reshape(1, CH), m2, guess)
    row = sds((1, CH), F32)
    full = sds((CH, 3 * TAPS), F32)
    g1, b1, g2, b2 = call(
        lambda *refs: unpack_kernel(total, *refs),
        (full, row, full, row),
        scratch=[pltpu.VMEM((total, 128), F32)],
        ins=[SM, VM, VM],
        mib=8,
    )(core, gathered, other)
    return (pred.reshape(1, CH, rows, NS), g1, b1.reshape(CH), g2, b2.reshape(CH))


def solution(mesh):
    wrap, samp = mesh.devices.shape
    split = Mesh(mesh.devices.reshape(wrap, samp // 2, 2), ("wrap", "x", "core"))
    field = P(("x", "core"), None, "wrap", None)
    return jax.shard_map(
        body,
        mesh=split,
        in_specs=(field, field, P(), P(), P(), P(), P()),
        out_specs=(field, P(), P(), P(), P()),
        check_vma=False,
    )
```
